256 devices in a mesh: seq: 128 (over y, x_hi, z, core), kv: 2 (over x_lo).
Axes of the slice: x: 4 (x_hi: 2, x_lo: 2; x = x_hi * 2 + x_lo), y: 4, z: 8, core: 2. Of those that a mesh axis runs over, the one named last changes fastest.
Arguments:
- queries: bfloat16 [32768, 32, 128], P('seq', 'kv'), may hold values from -6 to 6
- keys: bfloat16 [32768, 16, 128], P('seq', 'kv'), may hold values from -6 to 6
- values: bfloat16 [32768, 16, 128], P('seq', 'kv'), may hold values from -6 to 6
- output_gradient: bfloat16 [32768, 32, 128], P('seq', 'kv'), may hold values from -288 to 288
- window_start: int32 [32768], P('seq'), may hold values from 0 to 32767, as said below
- query_gain: float32 [128], replicated, may hold values from 0.1 to 1.9
- key_gain: float32 [128], replicated, may hold values from 0.1 to 1.9
Outputs:
- query_grad: bfloat16 [32768, 32, 128], P('seq', 'kv')
- key_grad: bfloat16 [32768, 16, 128], P('seq', 'kv')
- value_grad: bfloat16 [32768, 16, 128], P('seq', 'kv')
- query_gain_grad: float32 [128], replicated
- key_gain_grad: float32 [128], replicated
The draws below stay inside these ranges and needn't reach their ends.
Inputs may be any that keep to these rules, and one draw needn't show every extreme that they name: window_start[t] = max(first position of token t's document, t - 1023); documents are runs of consecutive tokens, the last token begins a document of its own, and t - window_start[t] equals 1023 for some token.
All inputs are finite; a program needn't handle non-finite values.
Results may differ from the reference program's by a relative error of at most 0.014.
Values may be sent and summed in bfloat16 or wider, within the bound.
No kernel may reach another device: no remote copies, remote signals or barrier semaphores. Data moves between devices by JAX's collectives and lax.ppermute only.
A program may use at most 128 MiB of HBM per device.

```python
import jax
import jax.numpy as jnp
from jax import lax

QUERY_HEAD_COUNT = 32
KEY_VALUE_HEADS = 16
HEAD_SIZE = 128
WINDOW_LENGTH = 1024
SHARD_TOKENS = 256
SLAB_TOKENS = 32768
N_SEQ = 128


grad_level = 16.0


def draw_window_start(key, part):
    position = jnp.arange(SLAB_TOKENS, dtype=jnp.int32)
    marker = jax.random.randint(jax.random.fold_in(key, 11), (SLAB_TOKENS,), 0, 3 * WINDOW_LENGTH)
    begins = (marker == 0) & (position > WINDOW_LENGTH) | (position == 0) | (position == SLAB_TOKENS - 1)
    doc_first = lax.cummax(jnp.where(begins, position, 0), axis=0)
    return jnp.maximum(doc_first, position - WINDOW_LENGTH + 1).astype(jnp.int32)


def draw_output_gradient(key, part):
    full_shape = (SLAB_TOKENS, QUERY_HEAD_COUNT, HEAD_SIZE)
    sample_key = jax.random.fold_in(key, 23)
    fraction = jnp.arange(SLAB_TOKENS, dtype=jnp.float32) / SLAB_TOKENS
    sample = jnp.clip(jax.random.normal(sample_key, full_shape, jnp.float32), -6.0, 6.0)
    scale_ramp = 1.0 + 2.0 * fraction
    return (grad_level * sample * scale_ramp[:, None, None]).astype(jnp.bfloat16)


def block_levels(stream_key, extent, shards, low, top_value):
    loudness, own = 1.0, jax.random.fold_in(stream_key, 6)
    for axis_at, blocks in shards:
        steps = jnp.exp(jax.random.uniform(jax.random.fold_in(own, axis_at), (blocks,), jnp.float32, low / len(shards), top_value / len(shards)))
        loudness = loudness * jnp.repeat(steps, extent[axis_at] // blocks).reshape([-1 if axis == axis_at else 1 for axis in range(len(extent))])
    return loudness


def centred(stream_key, shape, spread, reach, pieces=(), kind=jnp.bfloat16):
    level = block_levels(stream_key, shape, pieces, -0.22, 0.18) if pieces else 1.0
    drawn = jax.random.normal(stream_key, shape, jnp.float32) * spread * level
    return jnp.minimum(jnp.maximum(drawn, -reach), reach).astype(kind)


def setup_inputs(seed: int = 0) -> dict:
    arg_keys = jax.random.split(jax.random.key(seed), 8)
    return {
        "queries": centred(arg_keys[0], (SLAB_TOKENS, QUERY_HEAD_COUNT, HEAD_SIZE), 1.0, 6.0, ((0, 128), (1, 2))),
        "keys": centred(arg_keys[1], (SLAB_TOKENS, KEY_VALUE_HEADS, HEAD_SIZE), 1.0, 6.0, ((0, 128), (1, 2))),
        "values": centred(arg_keys[2], (SLAB_TOKENS, KEY_VALUE_HEADS, HEAD_SIZE), 1.0, 6.0, ((0, 128), (1, 2))),
        "output_gradient": draw_output_gradient(jax.random.fold_in(arg_keys[7], 71), 0),
        "window_start": draw_window_start(jax.random.fold_in(arg_keys[7], 71), 0),
        "query_gain": jnp.clip(1.0 + 0.18 * jax.random.normal(arg_keys[5], (HEAD_SIZE,), jnp.float32), 0.1, 1.9),
        "key_gain": jnp.clip(1.0 + 0.18 * jax.random.normal(arg_keys[6], (HEAD_SIZE,), jnp.float32), 0.1, 1.9),
    }


attn_scale = 168.0 ** (-0.5)
norm_eps = 1e-06
rope_base = 10000.0

def rotary_tables(positions, head_width):
    half_width = head_width // 2
    frequency = rope_base ** (-(jnp.arange(half_width, dtype=jnp.float32) * 2.0) / head_width)
    angles = positions.astype(jnp.float32)[:, None] * frequency[None, :]
    return (jnp.cos(angles)[:, None, :], jnp.sin(angles)[:, None, :])

def rotate(tensor, cos_table, sin_table):
    half_width = tensor.shape[-1] // 2
    first_half = tensor[..., :half_width]
    second_half = tensor[..., half_width:]
    return jnp.concatenate([first_half * cos_table - second_half * sin_table, second_half * cos_table + first_half * sin_table], axis=-1)

def unrotate(tensor, cos_table, sin_table):
    half_width = tensor.shape[-1] // 2
    first_half = tensor[..., :half_width]
    second_half = tensor[..., half_width:]
    return jnp.concatenate([first_half * cos_table + second_half * sin_table, second_half * cos_table - first_half * sin_table], axis=-1)

def normalize(tensor, gain_vec):
    tensor = tensor.astype(jnp.float32)
    inv_rms = lax.rsqrt(lax.optimization_barrier(jnp.mean(tensor * tensor, axis=-1, keepdims=True)) + norm_eps)
    unit_tensor = tensor * inv_rms
    return (unit_tensor, inv_rms, unit_tensor * gain_vec)

def norm_back(grad_norm, unit_tensor, inv_rms, gain_vec):
    grad_unit = grad_norm * gain_vec
    grad_tensor = inv_rms * (grad_unit - unit_tensor * lax.optimization_barrier(jnp.mean(grad_unit * unit_tensor, axis=-1, keepdims=True)))
    grad_gain = lax.optimization_barrier(jnp.sum(grad_norm * unit_tensor, axis=(0, 1)))
    return (grad_tensor, grad_gain)

def rounded(tensor):
    return lax.optimization_barrier(tensor.astype(jnp.bfloat16)).astype(jnp.float32)

def reference(queries, keys, values, output_gradient, window_start, query_gain, key_gain):
    positions = jnp.arange(SLAB_TOKENS, dtype=jnp.int32)
    cos_table, sin_table = rotary_tables(positions, HEAD_SIZE)
    query_unit, query_inv, query_normed = normalize(queries, query_gain)
    key_unit, key_inv, key_normed = normalize(keys, key_gain)
    rotated_query = rotate(query_normed, cos_table, sin_table).astype(jnp.bfloat16)
    rotated_key = rotate(key_normed, cos_table, sin_table).astype(jnp.bfloat16)
    group_count = QUERY_HEAD_COUNT // KEY_VALUE_HEADS
    reach_count = WINDOW_LENGTH // SHARD_TOKENS
    keys_padded_front = jnp.concatenate([jnp.zeros((WINDOW_LENGTH, KEY_VALUE_HEADS, HEAD_SIZE), jnp.bfloat16), rotated_key], axis=0)
    values_padded_front = jnp.concatenate([jnp.zeros((WINDOW_LENGTH, KEY_VALUE_HEADS, HEAD_SIZE), jnp.bfloat16), values], axis=0)
    span_rows = WINDOW_LENGTH + SHARD_TOKENS

    def block_step(carried, block_idx):
        key_sums, value_sums = carried
        first_row_index = (block_idx * SHARD_TOKENS).astype(jnp.int32)
        block_queries = lax.dynamic_slice_in_dim(rotated_query, first_row_index, SHARD_TOKENS, 0).reshape(SHARD_TOKENS, KEY_VALUE_HEADS, group_count, HEAD_SIZE).astype(jnp.float32)
        block_gradient = lax.dynamic_slice_in_dim(output_gradient, first_row_index, SHARD_TOKENS, 0).reshape(SHARD_TOKENS, KEY_VALUE_HEADS, group_count, HEAD_SIZE).astype(jnp.float32)
        key_block = lax.dynamic_slice_in_dim(keys_padded_front, first_row_index, span_rows, 0).astype(jnp.float32)
        value_block = lax.dynamic_slice_in_dim(values_padded_front, first_row_index, span_rows, 0).astype(jnp.float32)
        start_block = lax.dynamic_slice_in_dim(window_start, first_row_index, SHARD_TOKENS, 0)
        query_pos = first_row_index + jnp.arange(SHARD_TOKENS, dtype=jnp.int32)
        key_pos = first_row_index - WINDOW_LENGTH + jnp.arange(span_rows, dtype=jnp.int32)
        visible = (key_pos[None, :] >= start_block[:, None]) & (key_pos[None, :] <= query_pos[:, None])
        scores = attn_scale * jnp.einsum('tgrd,kgd->grtk', block_queries, key_block)
        exp_scores = jnp.where(visible, jnp.exp(scores), 0.0)
        row_total = lax.optimization_barrier(jnp.sum(exp_scores, axis=-1, keepdims=True))
        weights = exp_scores / row_total
        weights_b = weights.astype(jnp.bfloat16)
        weights_b = lax.optimization_barrier(weights_b).astype(jnp.float32)
        attended = jnp.einsum('grtk,kgd->grtd', weights_b, value_block)
        row_delta = lax.optimization_barrier(jnp.sum(jnp.transpose(block_gradient, (1, 2, 0, 3)) * attended, axis=-1))
        grad_weights = jnp.einsum('tgrd,kgd->grtk', block_gradient, value_block)
        grad_scores = (weights * (grad_weights - row_delta[..., None]) * attn_scale).astype(jnp.bfloat16)
        grad_scores = lax.optimization_barrier(grad_scores).astype(jnp.float32)
        query_part = jnp.einsum('grtk,kgd->tgrd', grad_scores, key_block)
        key_part = jnp.einsum('grtk,tgrd->kgd', grad_scores, block_queries)
        value_part = jnp.einsum('grtk,tgrd->kgd', weights_b, block_gradient)
        for index in range(reach_count + 1):
            target = (first_row_index + index * SHARD_TOKENS).astype(jnp.int32)
            key_piece = key_part[index * SHARD_TOKENS:(index + 1) * SHARD_TOKENS]
            value_piece = value_part[index * SHARD_TOKENS:(index + 1) * SHARD_TOKENS]
            key_now = lax.dynamic_slice_in_dim(key_sums, target, SHARD_TOKENS, 0)
            value_now = lax.dynamic_slice_in_dim(value_sums, target, SHARD_TOKENS, 0)
            if index < reach_count:
                key_new = rounded(key_now + rounded(key_piece))
                value_new = rounded(value_now + rounded(value_piece))
            else:
                key_new = key_now + key_piece
                value_new = value_now + value_piece
            key_sums = lax.dynamic_update_slice_in_dim(key_sums, key_new, target, 0)
            value_sums = lax.dynamic_update_slice_in_dim(value_sums, value_new, target, 0)
        return ((key_sums, value_sums), query_part.reshape(SHARD_TOKENS, QUERY_HEAD_COUNT, HEAD_SIZE))
    blank_rows = jnp.zeros((WINDOW_LENGTH + SLAB_TOKENS, KEY_VALUE_HEADS, HEAD_SIZE), jnp.float32)
    (key_sums, value_sums), query_parts = lax.scan(block_step, (blank_rows, blank_rows), jnp.arange(N_SEQ, dtype=jnp.int32), reverse=True)
    query_rot_grad = query_parts.reshape(SLAB_TOKENS, QUERY_HEAD_COUNT, HEAD_SIZE)
    query_normed_grad = unrotate(query_rot_grad, cos_table, sin_table)
    query_grad, query_gain_grad = norm_back(query_normed_grad, query_unit, query_inv, query_gain)
    key_normed_grad = unrotate(key_sums[WINDOW_LENGTH:], cos_table, sin_table)
    key_grad, key_gain_grad = norm_back(key_normed_grad, key_unit, key_inv, key_gain)
    value_grad = value_sums[WINDOW_LENGTH:].astype(jnp.bfloat16)
    return (query_grad.astype(jnp.bfloat16), key_grad.astype(jnp.bfloat16), value_grad, query_gain_grad, key_gain_grad)
```

```python
import functools
import math

import jax
import jax.numpy as jnp
from jax import lax
from jax.experimental import pallas as pl
from jax.experimental.pallas import tpu as pltpu
from jax.sharding import PartitionSpec as P


WINDOW_LENGTH = 1024
CHUNKS = 2
attn_scale = 168.0 ** (-0.5)
norm_eps = 1e-06
rope_base = 10000.0
query_scale = attn_scale * math.log2(math.e)
VMEM_LIMIT = 60 * 1024 * 1024
HALF = 128
bf16 = jnp.bfloat16
f32 = jnp.float32


def hop(value, steps):
    count = lax.axis_size("seq")
    first, last = max(0, -steps), min(count, count - steps)
    return lax.ppermute(value, "seq", [(s, s + steps) for s in range(first, last)])


def swap(value):
    return lax.ppermute(value, "seq", [(s, s ^ 1) for s in range(lax.axis_size("seq"))])


def all_sum(value):
    count = lax.axis_size("seq") * lax.axis_size("kv")
    bits = [1 << i for i in range(count.bit_length() - 1)]
    order = [2, 4, 8, 16, 1, 32, 64, 128] if count == 256 else bits
    for i in range(0, len(order), 2):
        pair = order[i : i + 2]
        masks = pair + ([pair[0] ^ pair[1]] if len(pair) == 2 else [])
        parts = [
            lax.ppermute(value, ("seq", "kv"), [(s, s ^ m) for s in range(count)]) for m in masks
        ]
        value = functools.reduce(lambda a, b: a + b, parts, value)
    return value


def rope_tables(positions, width):
    half = width // 2
    frequency = rope_base ** (-(jnp.arange(half, dtype=f32) * 2.0) / width)
    angles = positions.astype(f32)[:, None] * frequency[None, :]
    cos, sin = jnp.cos(angles), jnp.sin(angles)
    return jnp.concatenate([cos, cos], -1), jnp.concatenate([-sin, sin], -1)


def turn(x, cos, sin):
    return x * cos + pltpu.roll(x, 64, 1) * sin


def unturn(x, cos, sin):
    return x * cos - pltpu.roll(x, 64, 1) * sin


def key_prep_kernel(k_ref, v_ref, gain_ref, cos_ref, sin_ref, *rest):
    out_refs, scr = rest[:-1], rest[-1]
    tokens, heads, width = k_ref.shape
    per = heads // len(out_refs)
    scr[0] = k_ref[...].astype(f32).reshape(tokens * heads, width)
    scr[1] = v_ref[...].astype(f32).reshape(tokens * heads, width)
    for head in range(heads):
        out = out_refs[head // per]
        x = scr[0, pl.ds(head, tokens, stride=heads), :]
        inv = lax.rsqrt(jnp.mean(x * x, axis=-1, keepdims=True) + norm_eps)
        x = x * inv * gain_ref[...]
        out[0, head % per] = turn(x, cos_ref[...], sin_ref[...]).astype(bf16)
        out[1, head % per] = scr[1, pl.ds(head, tokens, stride=heads), :].astype(bf16)


def query_prep_kernel(q_ref, g_ref, start_ref, gain_ref, cos_ref, sin_ref, qs_ref, go_ref, bias_ref, scr):
    tokens, heads, width = q_ref.shape
    scr[0] = q_ref[...].astype(f32).reshape(tokens * heads, width)
    scr[1] = g_ref[...].astype(f32).reshape(tokens * heads, width)

    def one(group, carry):
        for r in range(2):
            x = scr[0, pl.ds(2 * group + r, tokens, stride=heads), :]
            inv = lax.rsqrt(jnp.mean(x * x, axis=-1, keepdims=True) + norm_eps)
            x = x * inv * gain_ref[...]
            x = (turn(x, cos_ref[...], sin_ref[...]) * query_scale).astype(bf16)
            g = scr[1, pl.ds(2 * group + r, tokens, stride=heads), :].astype(bf16)
            for h in range(tokens // HALF):
                qs_ref[group, h, r * HALF : (r + 1) * HALF, :] = x[h * HALF : (h + 1) * HALF]
                go_ref[group, h, r * HALF : (r + 1) * HALF, :] = g[h * HALF : (h + 1) * HALF]
        return carry

    lax.fori_loop(0, heads // 2, one, 0)
    span = bias_ref.shape[1]
    for h in range(tokens // HALF):
        key = lax.broadcasted_iota(jnp.int32, (span, HALF), 0) + h * HALF
        token = lax.broadcasted_iota(jnp.int32, (span, HALF), 1) + h * HALF
        seen = (key >= start_ref[h : h + 1, :]) & (key <= token + WINDOW_LENGTH)
        bias_ref[h] = jnp.where(seen, 0.0, -1e30).astype(f32)


NT = (((1,), (1,)), ((), ()))


def dot(a, b, dims=(((1,), (0,)), ((), ()))):
    return lax.dot_general(a, b, dims, preferred_element_type=f32)


def main_kernel(
    b4, b3, b2, b1, b0, q_ref, g_ref, bias_ref, cos_ref, sin_ref,
    odd_ref, even_ref, own_ref, dq_ref, gain_ref,
    k_scr, v_scr, kt_scr, e_scr, p_scr, dk_scr, dv_scr,
):
    tokens = b0.shape[2]
    blocks = (b4, b3, b2, b1, b0)
    for i, block in enumerate(blocks):
        k_scr[i * tokens : (i + 1) * tokens, :] = block[0, 0]
        v_scr[i * tokens : (i + 1) * tokens, :] = block[1, 0]
    kt_scr[...] = k_scr[...].astype(f32).T.astype(bf16)
    dk_scr[...] = jnp.zeros_like(dk_scr)
    dv_scr[...] = jnp.zeros_like(dv_scr)
    span = bias_ref.shape[1]
    step = 384
    steps = span // step

    @pl.when(pl.program_id(0) == 0)
    def _():
        gain_ref[...] = jnp.zeros_like(gain_ref)

    def unit(h, carry):
        base = pl.multiple_of(h * HALF, HALF)
        q = q_ref[0, h]
        g = g_ref[0, h]
        total = jnp.zeros((1, 2 * HALF), f32)
        delta = jnp.zeros((1, 2 * HALF), f32)
        for j in range(steps):
            rows = pl.ds(base + j * step, step)
            s = dot(k_scr[rows, :], q, NT)
            bias = bias_ref[h, j * step : (j + 1) * step, :]
            e = jnp.exp2(s + jnp.concatenate([bias, bias], 1))
            p = dot(v_scr[rows, :], g, NT)
            total = total + jnp.sum(e, axis=0, keepdims=True)
            delta = delta + jnp.sum(e * p, axis=0, keepdims=True)
            e_scr[j * step : (j + 1) * step, :] = e
            p_scr[j * step : (j + 1) * step, :] = p
        inv = 1.0 / total
        delta = delta * inv
        dqt = jnp.zeros((128, 2 * HALF), f32)
        for j in range(steps):
            rows = pl.ds(base + j * step, step)
            w = e_scr[j * step : (j + 1) * step, :] * inv
            ds = (w * (p_scr[j * step : (j + 1) * step, :] - delta)).astype(bf16)
            dk_scr[rows, :] += dot(ds, q)
            dv_scr[rows, :] += dot(w.astype(bf16), g)
            dqt = dqt + dot(kt_scr[:, rows], ds)
        dq = (dqt * attn_scale).T
        place = pl.ds(4 * 2 * HALF + base, HALF)
        cos = jnp.concatenate([cos_ref[place, :]] * 2, 0)
        sin = jnp.concatenate([sin_ref[place, :]] * 2, 0)
        dqn = unturn(dq, cos, sin)
        dq_ref[0, h] = dqn
        qn = unturn(q.astype(f32), cos, sin)
        gain_ref[0:1, :] += jnp.sum(dqn * qn, axis=0, keepdims=True)
        return carry

    lax.fori_loop(0, tokens // HALF, unit, 0)

    def finish(i):
        rows = slice(i * tokens, (i + 1) * tokens)
        dk = dk_scr[rows, :] * math.log(2.0)
        cos, sin = cos_ref[rows, :], sin_ref[rows, :]
        kn = unturn(k_scr[rows, :].astype(f32), cos, sin)
        gain_ref[1:2, :] += jnp.sum(unturn(dk, cos, sin) * kn, axis=0, keepdims=True)
        return dk, dv_scr[rows, :]

    for i, (ref, at) in enumerate(((even_ref, 0), (odd_ref, 0), (even_ref, 1), (odd_ref, 1))):
        dk, dv = finish(i)
        ref[at, 0, 0] = dk.astype(bf16)
        ref[at, 1, 0] = dv.astype(bf16)
    dk, dv = finish(4)
    own_ref[0, 0] = dk
    own_ref[1, 0] = dv


def norm_back(dn, x, gain):
    inv = lax.rsqrt(jnp.mean(x * x, axis=-1, keepdims=True) + norm_eps)
    unit = x * inv
    gu = dn * gain
    return inv * (gu - unit * jnp.mean(gu * unit, axis=-1, keepdims=True))


def query_end_kernel(q_ref, gain_ref, *rest):
    dq_refs, out_ref, scr, res = rest[:-3], rest[-3], rest[-2], rest[-1]
    tokens, heads, width = q_ref.shape
    scr[...] = q_ref[...].astype(f32).reshape(tokens * heads, width)
    per = dq_refs[0].shape[0]
    for c, dq_ref in enumerate(dq_refs):

        def one(i, carry, c=c, dq_ref=dq_ref):
            for r in range(2):
                rows = pl.ds(2 * (c * per + i) + r, tokens, stride=heads)
                dn = jnp.concatenate(
                    [dq_ref[i, h, r * HALF : (r + 1) * HALF, :] for h in range(tokens // HALF)], 0
                )
                res[rows, :] = norm_back(dn, scr[rows, :], gain_ref[...])
            return carry

        lax.fori_loop(0, per, one, 0)
    out_ref[...] = res[...].reshape(tokens, heads, width).astype(bf16)


def key_end_kernel(low_ref, k_ref, gain_ref, cos_ref, sin_ref, *rest):
    kg_ref, vg_ref, scr, res = rest[-4:]
    parts = rest[:-4]
    tokens, heads, width = k_ref.shape
    scr[...] = k_ref[...].astype(f32).reshape(tokens * heads, width)
    per = parts[0].shape[1]
    low = low_ref[0]
    for c in range(len(parts) // 3):
        own, other, came = parts[3 * c : 3 * c + 3]
        for i in range(per):
            rows = pl.ds(c * per + i, tokens, stride=heads)
            dk = own[0, i] + other[0, 0, i].astype(f32) * low + came[0, i].astype(f32)
            dn = unturn(dk, cos_ref[...], sin_ref[...])
            res[0, rows, :] = norm_back(dn, scr[rows, :], gain_ref[...])
            res[1, rows, :] = own[1, i] + other[0, 1, i].astype(f32) * low + came[1, i].astype(f32)
    kg_ref[...] = res[0].reshape(tokens, heads, width).astype(bf16)
    vg_ref[...] = res[1].reshape(tokens, heads, width).astype(bf16)


def params():
    return pltpu.CompilerParams(vmem_limit_bytes=VMEM_LIMIT)


def whole(kernel, outs, scratch, flops, bytes_accessed):
    return pl.pallas_call(
        kernel,
        out_shape=outs,
        scratch_shapes=scratch,
        compiler_params=params(),
        cost_estimate=pl.CostEstimate(
            flops=flops, bytes_accessed=bytes_accessed, transcendentals=0
        ),
    )


def body(queries, keys, values, output_gradient, window_start, query_gain, key_gain):
    tokens, heads, width = queries.shape
    groups = keys.shape[1]
    per = groups // CHUNKS
    reach = WINDOW_LENGTH // tokens
    span = WINDOW_LENGTH + HALF
    index = lax.axis_index("seq")
    core = lax.rem(index, 2)
    first = index * tokens
    low = core == 0
    positions = first - WINDOW_LENGTH + jnp.arange(WINDOW_LENGTH + tokens, dtype=jnp.int32)
    cos_all, sin_all = rope_tables(positions, width)
    cos_own, sin_own = rope_tables(first + jnp.arange(tokens, dtype=jnp.int32), width)
    sds = jax.ShapeDtypeStruct
    mib = 1 << 20

    own = list(whole(
        key_prep_kernel,
        [sds((2, per, tokens, width), bf16)] * CHUNKS,
        [pltpu.VMEM((2, tokens * groups, width), f32)],
        8 * mib, 2 * mib,
    )(keys, values, key_gain[None, :], cos_own, sin_own))
    near, far, side1, side3 = [], [], [], []
    for c in range(CHUNKS):
        near.append(hop(own[c], 2))
        far.append(hop(near[c], 2))
        side1.append(swap(jnp.where(low, own[c], near[c])))
        side3.append(swap(jnp.where(low, near[c], far[c])))

    starts = (window_start - first + WINDOW_LENGTH).reshape(tokens // HALF, HALF)
    qs, go, bias = whole(
        query_prep_kernel,
        [
            sds((groups, tokens // HALF, 2 * HALF, width), bf16),
            sds((groups, tokens // HALF, 2 * HALF, width), bf16),
            sds((tokens // HALF, span, HALF), f32),
        ],
        [pltpu.VMEM((2, tokens * heads, width), f32)],
        16 * mib, 5 * mib,
    )(queries, output_gradient, starts, query_gain[None, :], cos_own, sin_own)

    full = tokens * (reach + 1)
    kv_spec = pl.BlockSpec((2, 1, tokens, width), lambda i: (0, i, 0, 0))
    term_spec = pl.BlockSpec((2, 2, 1, tokens, width), lambda i: (0, 0, i, 0, 0))

    def at_rest(shape):
        return pl.BlockSpec(shape, lambda i: (0,) * len(shape))

    gains = jnp.zeros((2, width), f32)
    dqs, ends = [], []
    last = None
    for c in range(CHUNKS):
        if last is None:
            far[0], near[-1] = lax.optimization_barrier((far[0], near[-1]))
        else:
            own[c], last = lax.optimization_barrier((own[c], last))
        q_spec = pl.BlockSpec(
            (1, tokens // HALF, 2 * HALF, width), lambda i, c=c: (c * per + i, 0, 0, 0)
        )
        call = pl.pallas_call(
            main_kernel,
            grid=(per,),
            in_specs=[kv_spec] * 5
            + [q_spec] * 2
            + [
                at_rest((tokens // HALF, span, HALF)),
                at_rest((full, width)),
                at_rest((full, width)),
            ],
            out_specs=[
                term_spec,
                term_spec,
                kv_spec,
                pl.BlockSpec((1, tokens // HALF, 2 * HALF, width), lambda i: (i, 0, 0, 0)),
                at_rest((2, width)),
            ],
            out_shape=[
                sds((2, 2, per, tokens, width), bf16),
                sds((2, 2, per, tokens, width), bf16),
                sds((2, per, tokens, width), f32),
                sds((per, tokens // HALF, 2 * HALF, width), f32),
                sds((2, width), f32),
            ],
            scratch_shapes=[
                pltpu.VMEM((full, width), bf16),
                pltpu.VMEM((full, width), bf16),
                pltpu.VMEM((width, full), bf16),
                pltpu.VMEM((span, 2 * HALF), f32),
                pltpu.VMEM((span, 2 * HALF), f32),
                pltpu.VMEM((full, width), f32),
                pltpu.VMEM((full, width), f32),
            ],
            compiler_params=params(),
            cost_estimate=pl.CostEstimate(
                flops=2 * per * 2 * 5 * span * 2 * HALF * width * 2,
                bytes_accessed=per * 2 * mib,
                transcendentals=per * 2 * span * 2 * HALF,
            ),
            name="attention",
        )
        odd, even, mine, dq, gain = call(
            far[c], side3[c], near[c], side1[c], own[c], qs, go, bias, cos_all, sin_all
        )
        gains = gains + gain
        dqs.append(dq)
        other = swap(odd)
        send_far = even[0] + jnp.where(low, jnp.zeros_like(other[0]), other[0])
        came_far = hop(send_far, -2)
        send_near = even[1] + jnp.where(low, other[0], other[1]) + came_far
        ends += [mine, other, hop(send_near, -2)]
        last = send_far

    factor = jnp.stack([1.0 / (query_gain * query_scale), 1.0 / key_gain])
    gains = all_sum(gains * factor)

    call = whole(
        query_end_kernel,
        sds((tokens, heads, width), bf16),
        [pltpu.VMEM((tokens * heads, width), f32)] * 2,
        16 * mib, 4 * mib,
    )
    query_grad = call(queries, query_gain[None, :], *dqs)
    tile = 64
    token_spec = pl.BlockSpec((tile, groups, width), lambda i: (i, 0, 0))
    part_spec = pl.BlockSpec((2, per, tile, width), lambda i: (0, 0, i, 0))
    other_spec = pl.BlockSpec((1, 2, per, tile, width), lambda i: (1, 0, 0, i, 0))
    row_spec = pl.BlockSpec((tile, width), lambda i: (i, 0))
    key_grad, value_grad = pl.pallas_call(
        key_end_kernel,
        grid=(tokens // tile,),
        in_specs=[
            pl.BlockSpec(memory_space=pltpu.SMEM),
            token_spec,
            at_rest((1, width)),
            row_spec,
            row_spec,
        ]
        + [part_spec, other_spec, part_spec] * CHUNKS,
        out_specs=[token_spec] * 2,
        out_shape=[sds((tokens, groups, width), bf16)] * 2,
        scratch_shapes=[
            pltpu.VMEM((tile * groups, width), f32),
            pltpu.VMEM((2, tile * groups, width), f32),
        ],
        compiler_params=params(),
        cost_estimate=pl.CostEstimate(flops=8 * mib, bytes_accessed=4 * mib, transcendentals=0),
        name="key_end",
    )(low.astype(f32)[None], keys, key_gain[None, :], cos_own, sin_own, *ends)
    return query_grad, key_grad, value_grad, gains[0], gains[1]


def solution(mesh):
    wide = P("seq", "kv", None)
    return jax.shard_map(
        body,
        mesh=mesh,
        in_specs=(wide, wide, wide, wide, P("seq"), P(), P()),
        out_specs=(wide, wide, wide, P(), P()),
        check_vma=False,
    )
```

```python
import functools
import math

import jax
import jax.numpy as jnp
import numpy as np
from jax import lax
from jax.experimental import pallas as pl
from jax.experimental.pallas import tpu as pltpu
from jax.sharding import PartitionSpec as P


WINDOW_LENGTH = 1024
SPLIT = (4, 4)
TILE = 64
attn_scale = 168.0 ** (-0.5)
norm_eps = 1e-06
rope_base = 10000.0
query_scale = attn_scale * math.log2(math.e)
VMEM_LIMIT = 60 * 1024 * 1024
HALF = 128
bf16 = jnp.bfloat16
f32 = jnp.float32


def hop(value, steps):
    count = lax.axis_size("seq")
    first, last = max(0, -steps), min(count, count - steps)
    return lax.ppermute(value, "seq", [(s, s + steps) for s in range(first, last)])


def swap(value, cores=(0, 1)):
    pairs = [(s, s ^ 1) for s in range(lax.axis_size("seq")) if s % 2 in cores]
    return lax.ppermute(value, "seq", pairs)


def sum_rounds(count):
    if count != 256:
        return [[[s ^ (1 << i) for s in range(count)]] for i in range(count.bit_length() - 1)]

    def flip(*masks):
        return [[s ^ m for s in range(count)] for m in masks]

    def ahead(steps):
        return [(s & ~28) | (((s >> 2) + steps) % 8 << 2) for s in range(count)]

    return [flip(1, 2, 3), [ahead(1), ahead(2), ahead(3)], flip(64, 128, 192), flip(16, 32, 48)]


def all_sum(value):
    count = lax.axis_size("seq") * lax.axis_size("kv")
    for targets in sum_rounds(count):
        parts = [lax.ppermute(value, ("seq", "kv"), list(enumerate(target))) for target in targets]
        value = functools.reduce(lambda a, b: a + b, parts, value)
    return value


def rope_tables(positions, width):
    half = width // 2
    lane = lax.rem(jnp.arange(width, dtype=jnp.int32), half).astype(f32)
    sign = jnp.where(jnp.arange(width) < half, -1.0, 1.0).astype(f32)
    frequency = rope_base ** (-(lane * 2.0) / width)
    angles = positions.astype(f32)[:, None] * frequency[None, :]
    return jnp.cos(angles), jnp.sin(angles) * sign


def shift_table(tokens, reach, width):
    lane = np.arange(width) % (width // 2)
    sign = np.where(np.arange(width) < width // 2, -1.0, 1.0)
    angle = tokens * np.arange(reach, -1, -1.0)[:, None] * rope_base ** (-2.0 * lane / width)
    table = np.stack([np.cos(angle), np.sin(angle) * sign], 1)
    return table.reshape(2 * (reach + 1), width).astype(np.float32)


def turn(x, cos, sin):
    return x * cos + pltpu.roll(x, 64, 1) * sin


def unturn(x, cos, sin):
    return x * cos - pltpu.roll(x, 64, 1) * sin


def key_prep_kernel(k_ref, v_ref, gain_ref, cos_ref, sin_ref, *rest):
    out_refs, scr = rest[:-1], rest[-1]
    tokens, heads, width = k_ref.shape
    scr[0] = k_ref[...].astype(f32).reshape(tokens * heads, width)
    scr[1] = v_ref[...].astype(f32).reshape(tokens * heads, width)
    head = 0
    for out in out_refs:
        for i in range(out.shape[1]):
            x = scr[0, pl.ds(head, tokens, stride=heads), :]
            inv = lax.rsqrt(jnp.mean(x * x, axis=-1, keepdims=True) + norm_eps)
            x = x * inv * gain_ref[...]
            out[0, i] = turn(x, cos_ref[...], sin_ref[...]).astype(bf16)
            out[1, i] = scr[1, pl.ds(head, tokens, stride=heads), :].astype(bf16)
            head += 1


def query_prep_kernel(q_ref, g_ref, start_ref, gain_ref, cos_ref, sin_ref, qs_ref, go_ref, bias_ref, scr):
    tokens, heads, width = q_ref.shape
    scr[0] = q_ref[...].astype(f32).reshape(tokens * heads, width)
    scr[1] = g_ref[...].astype(f32).reshape(tokens * heads, width)
    for group in range(heads // 2):
        for r in range(2):
            rows = pl.ds(2 * group + r, tokens, stride=heads)
            x = scr[0, rows, :]
            inv = lax.rsqrt(jnp.mean(x * x, axis=-1, keepdims=True) + norm_eps) * query_scale
            x = x * inv * gain_ref[...]
            qs_ref[group, 0, r] = turn(x, cos_ref[...], sin_ref[...]).astype(bf16)
            go_ref[group, 0, r] = scr[1, rows, :].astype(bf16)
    step = pl.program_id(0)
    per = HALF // tokens

    @pl.when(lax.rem(step, per) == 0)
    def _():
        offset = lax.div(step, per) * HALF
        shape = bias_ref.shape[1:]
        key = lax.broadcasted_iota(jnp.int32, shape, 0) + offset
        token = lax.broadcasted_iota(jnp.int32, shape, 1) + offset
        seen = (key >= start_ref[0]) & (key <= token + WINDOW_LENGTH)
        bias_ref[0] = jnp.where(seen, 0.0, -1e30).astype(f32)


NT = (((1,), (1,)), ((), ()))


def dot(a, b, dims=(((1,), (0,)), ((), ()))):
    return lax.dot_general(a, b, dims, preferred_element_type=f32)


def turned_sum(same, cross, cos, sin):
    kept = jnp.sum(same * cos * cos, axis=0, keepdims=True)
    moved = jnp.sum(same * sin * sin, axis=0, keepdims=True)
    mixed = jnp.sum(cross * cos * sin, axis=0, keepdims=True)
    return kept - mixed + pltpu.roll(moved + mixed, 64, 1)


def main_kernel(
    low_ref, far, near, own, side_own, side_near, side_far, q_ref, g_ref, bias_ref, cos_ref, sin_ref, shift_ref,
    odd_ref, even_ref, own_ref, dq_ref, gain_ref,
    k_scr, v_scr, kt_scr, e_scr, p_scr, ks_scr, kx_scr, qs_scr, qx_scr,
):
    tokens, width = own.shape[2:]
    reach = k_scr.shape[0] // tokens - 1

    def place(i, block):
        k_scr[i * tokens : (i + 1) * tokens, :] = block[0, 0]
        v_scr[i * tokens : (i + 1) * tokens, :] = block[1, 0]

    place(0, far)
    place(2, near)
    place(4, own)

    @pl.when(low_ref[0] == 1)
    def _():
        place(1, side_far)
        place(3, side_near)

    @pl.when(low_ref[0] == 0)
    def _():
        place(1, side_near)
        place(3, side_own)

    @pl.when(pl.program_id(0) == 0)
    def _():
        ks_scr[...] = jnp.zeros_like(ks_scr)
        kx_scr[...] = jnp.zeros_like(kx_scr)
        qs_scr[...] = jnp.zeros_like(qs_scr)
        qx_scr[...] = jnp.zeros_like(qx_scr)

    kt_scr[...] = k_scr[...].T
    span = bias_ref.shape[1]
    step = span // 3
    lanes = 2 * HALF
    q = q_ref[...].reshape(2 * lanes, width)
    g = g_ref[...].reshape(2 * lanes, width)
    invs, deltas = [], []
    for h in range(2):
        total = jnp.zeros((1, lanes), f32)
        delta = jnp.zeros((1, lanes), f32)
        for j in range(span // step):
            base = h * HALF + j * step
            s = dot(k_scr[base : base + step, :], q[h * lanes : (h + 1) * lanes], NT)
            bias = bias_ref[h, j * step : (j + 1) * step, :]
            e = jnp.exp2(s + jnp.concatenate([bias, bias], 1))
            p = dot(v_scr[base : base + step, :], g[h * lanes : (h + 1) * lanes], NT)
            total = total + jnp.sum(e, axis=0, keepdims=True)
            delta = delta + jnp.sum(e * p, axis=0, keepdims=True)
            e_scr[h, j * step : (j + 1) * step, :] = e
            p_scr[h, j * step : (j + 1) * step, :] = p
        inv = 1.0 / total
        invs.append(inv)
        deltas.append(delta * inv)

    def terms(h, first, rows):
        at = slice(first - h * HALF, first - h * HALF + rows)
        w = e_scr[h, at, :] * invs[h]
        ds = w * (p_scr[h, at, :] - deltas[h])
        return w.astype(bf16), ds.astype(bf16)

    refs = ((even_ref, 0), (odd_ref, 0), (even_ref, 1), (odd_ref, 1))
    dqs = [jnp.zeros((width, lanes), f32) for _ in range(2)]
    pieces = [(0, HALF, (0,))]
    pieces += [(first, HALF, (0, 1)) for first in range(HALF, span, HALF)]
    pieces += [(span, HALF, (1,))]
    for first, rows, halves in pieces:
        found = [terms(h, first, rows) for h in halves]
        w = jnp.concatenate([x[0] for x in found], 1)
        ds = jnp.concatenate([x[1] for x in found], 1)
        used = slice(halves[0] * lanes, (halves[-1] + 1) * lanes)
        dk = dot(ds, q[used])
        dv = dot(w, g[used])
        for h, x in zip(halves, found):
            dqs[h] = dqs[h] + dot(kt_scr[:, first : first + rows], x[1])
        at = slice(first, first + rows)
        k = k_scr[at, :].astype(f32)
        ks_scr[at, :] += dk * k
        kx_scr[at, :] += dk * pltpu.roll(k, 64, 1)
        block, inside = divmod(first, tokens)
        inner = slice(inside, inside + rows)
        dk = dk * math.log(2.0)
        if block < reach:
            ref, which = refs[block]
            ref[which, 0, 0, inner, :] = dk.astype(bf16)
            ref[which, 1, 0, inner, :] = dv.astype(bf16)
        else:
            own_ref[0, 0, inner, :] = dk
            own_ref[1, 0, inner, :] = dv
    for h in range(2):
        dq = (dqs[h] * attn_scale).T
        dq_ref[0, h] = dq.reshape(2, HALF, width)
        x = q[h * lanes : (h + 1) * lanes].astype(f32)
        at = slice(h * lanes, (h + 1) * lanes)
        qs_scr[at, :] += dq * x
        qx_scr[at, :] += dq * pltpu.roll(x, 64, 1)

    @pl.when(pl.program_id(0) == pl.num_programs(0) - 1)
    def _():
        query = jnp.zeros((1, width), f32)
        for h in range(2):
            rows = slice(h * HALF, (h + 1) * HALF)
            for r in range(2):
                at = slice(h * lanes + r * HALF, h * lanes + (r + 1) * HALF)
                query = query + turned_sum(
                    qs_scr[at, :], qx_scr[at, :], cos_ref[rows, :], sin_ref[rows, :]
                )
        key = jnp.zeros((1, width), f32)
        for i in range(reach + 1):
            cb, sb = shift_ref[2 * i : 2 * i + 1, :], shift_ref[2 * i + 1 : 2 * i + 2, :]
            cos = cos_ref[...] * cb + sin_ref[...] * sb
            sin = sin_ref[...] * cb - cos_ref[...] * sb
            at = slice(i * tokens, (i + 1) * tokens)
            key = key + turned_sum(ks_scr[at, :], kx_scr[at, :], cos, sin)
        gain_ref[0:1, :] = query
        gain_ref[1:2, :] = key * math.log(2.0)


def norm_back(dn, x, gain):
    inv = lax.rsqrt(jnp.mean(x * x, axis=-1, keepdims=True) + norm_eps)
    unit = x * inv
    gu = dn * gain
    return inv * (gu - unit * jnp.mean(gu * unit, axis=-1, keepdims=True))


def query_end_kernel(q_ref, gain_ref, cos_ref, sin_ref, *rest):
    dq_refs, out_ref, scr, res = rest[:-3], rest[-3], rest[-2], rest[-1]
    tokens, heads, width = q_ref.shape
    scr[...] = q_ref[...].astype(f32).reshape(tokens * heads, width)
    head = 0
    for dq_ref in dq_refs:
        for i in range(dq_ref.shape[0]):
            for r in range(2):
                rows = pl.ds(head, tokens, stride=heads)
                dn = unturn(dq_ref[i, 0, r], cos_ref[...], sin_ref[...])
                res[rows, :] = norm_back(dn, scr[rows, :], gain_ref[...])
                head += 1
    out_ref[...] = res[...].reshape(tokens, heads, width).astype(bf16)


def key_end_kernel(low_ref, k_ref, gain_ref, cos_ref, sin_ref, *rest):
    kg_ref, vg_ref, scr, res = rest[-4:]
    parts = rest[:-4]
    tokens, heads, width = k_ref.shape
    scr[...] = k_ref[...].astype(f32).reshape(tokens * heads, width)
    low = low_ref[0].astype(f32)
    head = 0
    for c in range(len(parts) // 3):
        own, other, came = parts[3 * c : 3 * c + 3]
        for i in range(own.shape[1]):
            rows = pl.ds(head, tokens, stride=heads)
            dk = own[0, i] + other[0, 0, i].astype(f32) * low + came[0, i].astype(f32)
            dn = unturn(dk, cos_ref[...], sin_ref[...])
            res[0, rows, :] = norm_back(dn, scr[rows, :], gain_ref[...])
            res[1, rows, :] = own[1, i] + other[0, 1, i].astype(f32) * low + came[1, i].astype(f32)
            head += 1
    kg_ref[...] = res[0].reshape(tokens, heads, width).astype(bf16)
    vg_ref[...] = res[1].reshape(tokens, heads, width).astype(bf16)


def call(kernel, grid, in_specs, out_specs, outs, scratch, cost):
    return pl.pallas_call(
        kernel,
        grid=(grid,),
        in_specs=in_specs,
        out_specs=out_specs,
        out_shape=outs,
        scratch_shapes=scratch,
        compiler_params=pltpu.CompilerParams(vmem_limit_bytes=VMEM_LIMIT),
        cost_estimate=pl.CostEstimate(flops=cost[0], bytes_accessed=cost[1], transcendentals=0),
    )


def at_rest(*shape):
    return pl.BlockSpec(shape, lambda i: (0,) * len(shape))


def body(queries, keys, values, output_gradient, window_start, query_gain, key_gain):
    tokens, heads, width = queries.shape
    groups = keys.shape[1]
    reach = WINDOW_LENGTH // tokens
    span = WINDOW_LENGTH + HALF
    full = WINDOW_LENGTH + tokens
    halves = tokens // HALF
    index = lax.axis_index("seq")
    first = index * tokens
    low = lax.rem(index, 2) == 0
    flag = low.astype(jnp.int32)[None]
    cos, sin = rope_tables(first + jnp.arange(tokens, dtype=jnp.int32), width)
    shift = jnp.asarray(shift_table(tokens, reach, width))
    sds = jax.ShapeDtypeStruct
    mib = 1 << 20
    smem = pl.BlockSpec(memory_space=pltpu.SMEM)
    row_spec = pl.BlockSpec((TILE, width), lambda i: (i, 0))
    kv_tile = pl.BlockSpec((TILE, groups, width), lambda i: (i, 0, 0))
    q_tile = pl.BlockSpec((TILE, heads, width), lambda i: (i, 0, 0))
    per_half = HALF // TILE

    def half_spec(count):
        return pl.BlockSpec(
            (count, 1, 2, TILE, width), lambda i: (0, i // per_half, 0, i % per_half, 0)
        )

    def part_spec(count):
        return pl.BlockSpec((2, count, TILE, width), lambda i: (0, 0, i, 0))

    own = call(
        key_prep_kernel,
        tokens // TILE,
        [kv_tile, kv_tile, at_rest(1, width), row_spec, row_spec],
        [part_spec(n) for n in SPLIT],
        [sds((2, n, tokens, width), bf16) for n in SPLIT],
        [pltpu.VMEM((2, TILE * groups, width), f32)],
        (8 * mib, 2 * mib),
    )(keys, values, key_gain[None, :], cos, sin)
    near, far, side_own, side_near, side_far = [], [], [], [], []
    for c in range(len(SPLIT)):
        near.append(hop(own[c], 2))
        far.append(hop(near[c], 2))
        side_own.append(swap(own[c], (0,)))
        side_near.append(swap(near[c]))
        side_far.append(swap(far[c], (1,)))

    starts = (window_start - first + WINDOW_LENGTH).reshape(halves, 1, HALF)
    qs, go, bias = call(
        query_prep_kernel,
        tokens // TILE,
        [
            q_tile,
            q_tile,
            pl.BlockSpec((1, 1, HALF), lambda i: (i // per_half, 0, 0)),
            at_rest(1, width),
            row_spec,
            row_spec,
        ],
        [
            half_spec(groups),
            half_spec(groups),
            pl.BlockSpec((1, span, HALF), lambda i: (i // per_half, 0, 0)),
        ],
        [sds((groups, halves, 2, HALF, width), bf16)] * 2 + [sds((halves, span, HALF), f32)],
        [pltpu.VMEM((2, TILE * heads, width), f32)],
        (16 * mib, 5 * mib),
    )(queries, output_gradient, starts, query_gain[None, :], cos, sin)

    kv_spec = pl.BlockSpec((2, 1, tokens, width), lambda i: (0, i, 0, 0))
    term_spec = pl.BlockSpec((2, 2, 1, tokens, width), lambda i: (0, 0, i, 0, 0))
    unit = (1, halves, 2, HALF, width)
    gains = jnp.zeros((2, width), f32)
    dqs, ends = [], []
    base = 0
    for c, per in enumerate(SPLIT):
        q_spec = pl.BlockSpec(unit, lambda i, base=base: (base + i, 0, 0, 0, 0))
        base += per
        attend = call(
            main_kernel,
            per,
            [smem]
            + [kv_spec] * 6
            + [q_spec] * 2
            + [at_rest(halves, span, HALF)]
            + [at_rest(tokens, width)] * 2
            + [at_rest(2 * (reach + 1), width)],
            [
                term_spec,
                term_spec,
                kv_spec,
                pl.BlockSpec(unit, lambda i: (i, 0, 0, 0, 0)),
                at_rest(2, width),
            ],
            [
                sds((2, 2, per, tokens, width), bf16),
                sds((2, 2, per, tokens, width), bf16),
                sds((2, per, tokens, width), f32),
                sds((per, *unit[1:]), f32),
                sds((2, width), f32),
            ],
            [
                pltpu.VMEM((full, width), bf16),
                pltpu.VMEM((full, width), bf16),
                pltpu.VMEM((width, full), bf16),
                pltpu.VMEM((halves, span, 2 * HALF), f32),
                pltpu.VMEM((halves, span, 2 * HALF), f32),
                pltpu.VMEM((full, width), f32),
                pltpu.VMEM((full, width), f32),
                pltpu.VMEM((2 * tokens, width), f32),
                pltpu.VMEM((2 * tokens, width), f32),
            ],
            (2 * per * 2 * 5 * span * 2 * HALF * width * 2, per * 2 * mib),
        )
        odd, even, mine, dq, gain = attend(
            flag, far[c], near[c], own[c], side_own[c], side_near[c], side_far[c],
            qs, go, bias, cos, sin, shift,
        )
        gains = gains + gain
        dqs.append(dq)
        other = swap(odd)
        send_far = even[0] + jnp.where(low, jnp.zeros_like(other[0]), other[0])
        came_far = hop(send_far, -2)
        send_near = even[1] + jnp.where(low, other[0], other[1]) + came_far
        ends += [mine, other, hop(send_near, -2)]

    factor = jnp.stack([1.0 / (query_gain * query_scale), 1.0 / key_gain])
    gains = all_sum(gains * factor)

    query_grad = call(
        query_end_kernel,
        tokens // TILE,
        [q_tile, at_rest(1, width), row_spec, row_spec] + [half_spec(n) for n in SPLIT],
        q_tile,
        sds((tokens, heads, width), bf16),
        [pltpu.VMEM((TILE * heads, width), f32)] * 2,
        (16 * mib, 4 * mib),
    )(queries, query_gain[None, :], cos, sin, *dqs)
    specs = []
    for n in SPLIT:
        other_spec = pl.BlockSpec((1, 2, n, TILE, width), lambda i: (1, 0, 0, i, 0))
        specs += [part_spec(n), other_spec, part_spec(n)]
    key_grad, value_grad = call(
        key_end_kernel,
        tokens // TILE,
        [smem, kv_tile, at_rest(1, width), row_spec, row_spec] + specs,
        [kv_tile] * 2,
        [sds((tokens, groups, width), bf16)] * 2,
        [
            pltpu.VMEM((TILE * groups, width), f32),
            pltpu.VMEM((2, TILE * groups, width), f32),
        ],
        (8 * mib, 4 * mib),
    )(flag, keys, key_gain[None, :], cos, sin, *ends)
    return query_grad, key_grad, value_grad, gains[0], gains[1]


def solution(mesh):
    wide = P("seq", "kv", None)
    return jax.shard_map(
        body,
        mesh=mesh,
        in_specs=(wide, wide, wide, wide, P("seq"), P(), P()),
        out_specs=(wide, wide, wide, P(), P()),
        check_vma=False,
    )
```

```python
import functools
import math

import jax
import jax.numpy as jnp
import numpy as np
from jax import lax
from jax.experimental import pallas as pl
from jax.experimental.pallas import tpu as pltpu
from jax.sharding import PartitionSpec as P


WINDOW_LENGTH = 1024
SPLIT = (4, 4)
TILE = 64
attn_scale = 168.0 ** (-0.5)
norm_eps = 1e-06
rope_base = 10000.0
query_scale = attn_scale * math.log2(math.e)
VMEM_LIMIT = 60 * 1024 * 1024
HALF = 128
bf16 = jnp.bfloat16
f32 = jnp.float32


def hop(value, steps):
    count = lax.axis_size("seq")
    first, last = max(0, -steps), min(count, count - steps)
    return lax.ppermute(value, "seq", [(s, s + steps) for s in range(first, last)])


def swap(value):
    return lax.ppermute(value, "seq", [(s, s ^ 1) for s in range(lax.axis_size("seq"))])


def sum_rounds(count):
    if count != 256:
        return [[[s ^ (1 << i) for s in range(count)]] for i in range(count.bit_length() - 1)]

    def flip(*masks):
        return [[s ^ m for s in range(count)] for m in masks]

    def ahead(steps):
        return [(s & ~28) | (((s >> 2) + steps) % 8 << 2) for s in range(count)]

    return [flip(1, 2, 3), [ahead(1), ahead(2), ahead(3)], flip(64, 128, 192), flip(16, 32, 48)]


def all_sum(value):
    count = lax.axis_size("seq") * lax.axis_size("kv")
    for targets in sum_rounds(count):
        parts = [lax.ppermute(value, ("seq", "kv"), list(enumerate(target))) for target in targets]
        value = functools.reduce(lambda a, b: a + b, parts, value)
    return value


def rope_tables(positions, width):
    half = width // 2
    lane = lax.rem(jnp.arange(width, dtype=jnp.int32), half).astype(f32)
    sign = jnp.where(jnp.arange(width) < half, -1.0, 1.0).astype(f32)
    frequency = rope_base ** (-(lane * 2.0) / width)
    angles = positions.astype(f32)[:, None] * frequency[None, :]
    return jnp.cos(angles), jnp.sin(angles) * sign


def shift_table(tokens, reach, width):
    lane = np.arange(width) % (width // 2)
    sign = np.where(np.arange(width) < width // 2, -1.0, 1.0)
    angle = tokens * np.arange(reach, -1, -1.0)[:, None] * rope_base ** (-2.0 * lane / width)
    table = np.stack([np.cos(angle), np.sin(angle) * sign], 1)
    return table.reshape(2 * (reach + 1), width).astype(np.float32)


def turn(x, cos, sin):
    return x * cos + pltpu.roll(x, 64, 1) * sin


def unturn(x, cos, sin):
    return x * cos - pltpu.roll(x, 64, 1) * sin


NT = (((1,), (1,)), ((), ()))


def dot(a, b, dims=(((1,), (0,)), ((), ()))):
    return lax.dot_general(a, b, dims, preferred_element_type=f32)


def row_mean(x):
    high = x.astype(bf16)
    rest = (x - high.astype(f32)).astype(bf16)
    share = jnp.full((x.shape[1], x.shape[1]), 1.0 / x.shape[1], bf16)
    return dot(high, share) + dot(rest, share)


def flat(ref):
    tokens, heads, width = ref.shape
    return ref[...].astype(f32).reshape(tokens * heads, width)


def inverse(x):
    return lax.rsqrt(row_mean(x * x) + norm_eps)


def key_prep_kernel(k_ref, v_ref, gain_ref, cos_ref, sin_ref, *rest):
    out_refs, scr = rest[:-1], rest[-1]
    tokens, heads, _ = k_ref.shape
    x = flat(k_ref)
    scr[0] = x * inverse(x) * gain_ref[...]
    scr[1] = flat(v_ref)
    cos, sin = cos_ref[...], sin_ref[...]
    head = 0
    for out in out_refs:
        for i in range(out.shape[1]):
            rows = pl.ds(head, tokens, stride=heads)
            out[0, i] = turn(scr[0, rows, :], cos, sin).astype(bf16)
            out[1, i] = scr[1, rows, :].astype(bf16)
            head += 1


def query_prep_kernel(
    first_ref, q_ref, g_ref, start_ref, gain_ref, cos_ref, sin_ref, qs_ref, go_ref, bias_ref, scr
):
    tokens, heads, _ = q_ref.shape
    x = flat(q_ref)
    scr[0] = x * inverse(x) * (gain_ref[...] * query_scale)
    scr[1] = flat(g_ref)
    cos, sin = cos_ref[...], sin_ref[...]
    for group in range(heads // 2):
        for r in range(2):
            rows = pl.ds(2 * group + r, tokens, stride=heads)
            qs_ref[group, 0, r] = turn(scr[0, rows, :], cos, sin).astype(bf16)
            go_ref[group, 0, r] = scr[1, rows, :].astype(bf16)
    step = pl.program_id(0)
    per = HALF // tokens

    @pl.when(lax.rem(step, per) == 0)
    def _():
        offset = lax.div(step, per) * HALF
        shape = bias_ref.shape[1:]
        key = lax.broadcasted_iota(jnp.int32, shape, 0) + offset
        token = lax.broadcasted_iota(jnp.int32, shape, 1) + offset
        start = start_ref[0] - first_ref[0] + WINDOW_LENGTH
        seen = (key >= start) & (key <= token + WINDOW_LENGTH)
        bias_ref[0] = jnp.where(seen, 0.0, -1e30).astype(f32)


def turned_sum(same, cross, cos, sin):
    kept = jnp.sum(same * cos * cos, axis=0, keepdims=True)
    moved = jnp.sum(same * sin * sin, axis=0, keepdims=True)
    mixed = jnp.sum(cross * cos * sin, axis=0, keepdims=True)
    return kept - mixed + pltpu.roll(moved + mixed, 64, 1)


def main_kernel(
    low_ref, far, near, own, side_own, side_near, side_far, q_ref, g_ref, bias_ref, cos_ref, sin_ref, shift_ref,
    odd_ref, even_ref, own_ref, dq_ref, gain_ref,
    k_scr, v_scr, kt_scr, e_scr, p_scr, ds_scr, ks_scr, kx_scr, qs_scr, qx_scr,
):
    tokens, width = own.shape[2:]
    reach = k_scr.shape[0] // tokens - 1

    def place(i, block):
        k_scr[i * tokens : (i + 1) * tokens, :] = block[0, 0]
        v_scr[i * tokens : (i + 1) * tokens, :] = block[1, 0]

    place(0, far)
    place(2, near)
    place(4, own)

    @pl.when(low_ref[0] == 1)
    def _():
        place(1, side_far)
        place(3, side_near)

    @pl.when(low_ref[0] == 0)
    def _():
        place(1, side_near)
        place(3, side_own)

    @pl.when(pl.program_id(0) == 0)
    def _():
        ks_scr[...] = jnp.zeros_like(ks_scr)
        kx_scr[...] = jnp.zeros_like(kx_scr)
        qs_scr[...] = jnp.zeros_like(qs_scr)
        qx_scr[...] = jnp.zeros_like(qx_scr)

    kt_scr[...] = k_scr[...].T
    span = bias_ref.shape[1]
    step = span // 3
    lanes = 2 * HALF
    q = q_ref[...].reshape(2 * lanes, width)
    g = g_ref[...].reshape(2 * lanes, width)
    invs, deltas = [], []
    for h in range(2):
        total = jnp.zeros((1, lanes), f32)
        delta = jnp.zeros((1, lanes), f32)
        for j in range(span // step):
            base = h * HALF + j * step
            s = dot(k_scr[base : base + step, :], q[h * lanes : (h + 1) * lanes], NT)
            bias = bias_ref[h, j * step : (j + 1) * step, :]
            e = jnp.exp2(s + jnp.concatenate([bias, bias], 1))
            p = dot(v_scr[base : base + step, :], g[h * lanes : (h + 1) * lanes], NT)
            total = total + jnp.sum(e, axis=0, keepdims=True)
            delta = delta + jnp.sum(e * p, axis=0, keepdims=True)
            e_scr[h, j * step : (j + 1) * step, :] = e
            p_scr[h, j * step : (j + 1) * step, :] = p
        inv = 1.0 / total
        invs.append(inv)
        deltas.append(delta * inv)

    def terms(h, first, rows):
        at = slice(first - h * HALF, first - h * HALF + rows)
        w = e_scr[h, at, :] * invs[h]
        ds = w * (p_scr[h, at, :] - deltas[h])
        return w.astype(bf16), ds.astype(bf16)

    refs = ((even_ref, 0), (odd_ref, 0), (even_ref, 1), (odd_ref, 1))
    pieces = [(0, HALF, (0,))]
    pieces += [(first, HALF, (0, 1)) for first in range(HALF, span, HALF)]
    pieces += [(span, HALF, (1,))]
    for first, rows, halves in pieces:
        found = [terms(h, first, rows) for h in halves]
        w = jnp.concatenate([x[0] for x in found], 1)
        ds = jnp.concatenate([x[1] for x in found], 1)
        used = slice(halves[0] * lanes, (halves[-1] + 1) * lanes)
        dk = dot(ds, q[used])
        dv = dot(w, g[used])
        for h, x in zip(halves, found):
            ds_scr[h, first - h * HALF : first - h * HALF + rows, :] = x[1]
        at = slice(first, first + rows)
        k = k_scr[at, :].astype(f32)
        ks_scr[at, :] += dk * k
        kx_scr[at, :] += dk * pltpu.roll(k, 64, 1)
        block, inside = divmod(first, tokens)
        inner = slice(inside, inside + rows)
        dk = dk * math.log(2.0)
        if block < reach:
            ref, which = refs[block]
            ref[which, 0, 0, inner, :] = dk.astype(bf16)
            ref[which, 1, 0, inner, :] = dv.astype(bf16)
        else:
            own_ref[0, 0, inner, :] = dk
            own_ref[1, 0, inner, :] = dv
    for h in range(2):
        dq = dot(kt_scr[:, h * HALF : h * HALF + span], ds_scr[h])
        dq = (dq * attn_scale).T
        dq_ref[0, h] = dq.reshape(2, HALF, width)
        x = q[h * lanes : (h + 1) * lanes].astype(f32)
        at = slice(h * lanes, (h + 1) * lanes)
        qs_scr[at, :] += dq * x
        qx_scr[at, :] += dq * pltpu.roll(x, 64, 1)

    @pl.when(pl.program_id(0) == pl.num_programs(0) - 1)
    def _():
        query = jnp.zeros((1, width), f32)
        for h in range(2):
            rows = slice(h * HALF, (h + 1) * HALF)
            for r in range(2):
                at = slice(h * lanes + r * HALF, h * lanes + (r + 1) * HALF)
                query = query + turned_sum(
                    qs_scr[at, :], qx_scr[at, :], cos_ref[rows, :], sin_ref[rows, :]
                )
        key = jnp.zeros((1, width), f32)
        for i in range(reach + 1):
            cb, sb = shift_ref[2 * i : 2 * i + 1, :], shift_ref[2 * i + 1 : 2 * i + 2, :]
            cos = cos_ref[...] * cb + sin_ref[...] * sb
            sin = sin_ref[...] * cb - cos_ref[...] * sb
            at = slice(i * tokens, (i + 1) * tokens)
            key = key + turned_sum(ks_scr[at, :], kx_scr[at, :], cos, sin)
        gain_ref[0:1, :] = query
        gain_ref[1:2, :] = key * math.log(2.0)


def norm_back(x, scaled):
    inv = inverse(x)
    unit = x * inv
    return inv * (scaled - unit * row_mean(scaled * unit))


def query_end_kernel(q_ref, gain_ref, cos_ref, sin_ref, *rest):
    dq_refs, out_ref, scr = rest[:-2], rest[-2], rest[-1]
    tokens, heads, width = q_ref.shape
    cos, sin, gain = cos_ref[...], sin_ref[...], gain_ref[...]
    head = 0
    for dq_ref in dq_refs:
        for i in range(dq_ref.shape[0]):
            for r in range(2):
                rows = pl.ds(head, tokens, stride=heads)
                scr[rows, :] = unturn(dq_ref[i, 0, r], cos, sin) * gain
                head += 1
    out_ref[...] = norm_back(flat(q_ref), scr[...]).reshape(tokens, heads, width).astype(bf16)


def key_end_kernel(low_ref, k_ref, gain_ref, cos_ref, sin_ref, *rest):
    kg_ref, vg_ref, scr = rest[-3:]
    parts = rest[:-3]
    tokens, heads, width = k_ref.shape
    low = low_ref[0].astype(f32)
    cos, sin, gain = cos_ref[...], sin_ref[...], gain_ref[...]
    head = 0
    for c in range(len(parts) // 3):
        own, other, came = parts[3 * c : 3 * c + 3]
        for i in range(own.shape[1]):
            rows = pl.ds(head, tokens, stride=heads)
            dk = own[0, i] + other[0, 0, i].astype(f32) * low + came[0, i].astype(f32)
            scr[0, rows, :] = unturn(dk, cos, sin) * gain
            scr[1, rows, :] = own[1, i] + other[0, 1, i].astype(f32) * low + came[1, i].astype(f32)
            head += 1
    kg_ref[...] = norm_back(flat(k_ref), scr[0]).reshape(tokens, heads, width).astype(bf16)
    vg_ref[...] = scr[1].reshape(tokens, heads, width).astype(bf16)


def call(kernel, grid, in_specs, out_specs, outs, scratch, cost):
    return pl.pallas_call(
        kernel,
        grid=(grid,),
        in_specs=in_specs,
        out_specs=out_specs,
        out_shape=outs,
        scratch_shapes=scratch,
        compiler_params=pltpu.CompilerParams(vmem_limit_bytes=VMEM_LIMIT),
        cost_estimate=pl.CostEstimate(flops=cost[0], bytes_accessed=cost[1], transcendentals=0),
    )


def at_rest(*shape):
    return pl.BlockSpec(shape, lambda i: (0,) * len(shape))


def body(queries, keys, values, output_gradient, window_start, query_gain, key_gain):
    tokens, heads, width = queries.shape
    groups = keys.shape[1]
    reach = WINDOW_LENGTH // tokens
    span = WINDOW_LENGTH + HALF
    full = WINDOW_LENGTH + tokens
    halves = tokens // HALF
    index = lax.axis_index("seq")
    first = index * tokens
    low = lax.rem(index, 2) == 0
    flag = low.astype(jnp.int32)[None]
    cos, sin = rope_tables(first + jnp.arange(tokens, dtype=jnp.int32), width)
    shift = jnp.asarray(shift_table(tokens, reach, width))
    sds = jax.ShapeDtypeStruct
    mib = 1 << 20
    smem = pl.BlockSpec(memory_space=pltpu.SMEM)
    row_spec = pl.BlockSpec((TILE, width), lambda i: (i, 0))
    kv_tile = pl.BlockSpec((TILE, groups, width), lambda i: (i, 0, 0))
    q_tile = pl.BlockSpec((TILE, heads, width), lambda i: (i, 0, 0))
    per_half = HALF // TILE

    def half_spec(count):
        return pl.BlockSpec(
            (count, 1, 2, TILE, width), lambda i: (0, i // per_half, 0, i % per_half, 0)
        )

    def part_spec(count):
        return pl.BlockSpec((2, count, TILE, width), lambda i: (0, 0, i, 0))

    own = call(
        key_prep_kernel,
        tokens // TILE,
        [kv_tile, kv_tile, at_rest(1, width), row_spec, row_spec],
        [part_spec(n) for n in SPLIT],
        [sds((2, n, tokens, width), bf16) for n in SPLIT],
        [pltpu.VMEM((2, TILE * groups, width), f32)],
        (8 * mib, 2 * mib),
    )(keys, values, key_gain[None, :], cos, sin)
    near, far, side_own, side_near, side_far = [], [], [], [], []
    for c in range(len(SPLIT)):
        near.append(hop(own[c], 2))
        far.append(hop(near[c], 2))
        side_own.append(swap(own[c]))
        side_near.append(swap(near[c]))
        side_far.append(swap(far[c]))

    starts = window_start.reshape(halves, 1, HALF)
    qs, go, bias = call(
        query_prep_kernel,
        tokens // TILE,
        [
            smem,
            q_tile,
            q_tile,
            pl.BlockSpec((1, 1, HALF), lambda i: (i // per_half, 0, 0)),
            at_rest(1, width),
            row_spec,
            row_spec,
        ],
        [
            half_spec(groups),
            half_spec(groups),
            pl.BlockSpec((1, span, HALF), lambda i: (i // per_half, 0, 0)),
        ],
        [sds((groups, halves, 2, HALF, width), bf16)] * 2 + [sds((halves, span, HALF), f32)],
        [pltpu.VMEM((2, TILE * heads, width), f32)],
        (16 * mib, 5 * mib),
    )(first.astype(jnp.int32)[None], queries, output_gradient, starts, query_gain[None, :], cos, sin)

    kv_spec = pl.BlockSpec((2, 1, tokens, width), lambda i: (0, i, 0, 0))
    term_spec = pl.BlockSpec((2, 2, 1, tokens, width), lambda i: (0, 0, i, 0, 0))
    unit = (1, halves, 2, HALF, width)
    gains = jnp.zeros((2, width), f32)
    dqs, ends = [], []
    base = 0
    for c, per in enumerate(SPLIT):
        q_spec = pl.BlockSpec(unit, lambda i, base=base: (base + i, 0, 0, 0, 0))
        base += per
        attend = call(
            main_kernel,
            per,
            [smem]
            + [kv_spec] * 6
            + [q_spec] * 2
            + [at_rest(halves, span, HALF)]
            + [at_rest(tokens, width)] * 2
            + [at_rest(2 * (reach + 1), width)],
            [
                term_spec,
                term_spec,
                kv_spec,
                pl.BlockSpec(unit, lambda i: (i, 0, 0, 0, 0)),
                at_rest(2, width),
            ],
            [
                sds((2, 2, per, tokens, width), bf16),
                sds((2, 2, per, tokens, width), bf16),
                sds((2, per, tokens, width), f32),
                sds((per, *unit[1:]), f32),
                sds((2, width), f32),
            ],
            [
                pltpu.VMEM((full, width), bf16),
                pltpu.VMEM((full, width), bf16),
                pltpu.VMEM((width, full), bf16),
                pltpu.VMEM((halves, span, 2 * HALF), f32),
                pltpu.VMEM((halves, span, 2 * HALF), f32),
                pltpu.VMEM((halves, span, 2 * HALF), bf16),
                pltpu.VMEM((full, width), f32),
                pltpu.VMEM((full, width), f32),
                pltpu.VMEM((2 * tokens, width), f32),
                pltpu.VMEM((2 * tokens, width), f32),
            ],
            (2 * per * 2 * 5 * span * 2 * HALF * width * 2, per * 2 * mib),
        )
        odd, even, mine, dq, gain = attend(
            flag, far[c], near[c], own[c], side_own[c], side_near[c], side_far[c],
            qs, go, bias, cos, sin, shift,
        )
        gains = gains + gain
        dqs.append(dq)
        other = swap(odd)
        send_far = even[0] + jnp.where(low, jnp.zeros_like(other[0]), other[0])
        came_far = hop(send_far, -2)
        send_near = even[1] + jnp.where(low, other[0], other[1]) + came_far
        ends += [mine, other, hop(send_near, -2)]

    factor = jnp.stack([1.0 / (query_gain * query_scale), 1.0 / key_gain])
    gains = all_sum(gains * factor)

    query_grad = call(
        query_end_kernel,
        tokens // TILE,
        [q_tile, at_rest(1, width), row_spec, row_spec] + [half_spec(n) for n in SPLIT],
        q_tile,
        sds((tokens, heads, width), bf16),
        [pltpu.VMEM((TILE * heads, width), f32)],
        (16 * mib, 4 * mib),
    )(queries, query_gain[None, :], cos, sin, *dqs)
    specs = []
    for n in SPLIT:
        other_spec = pl.BlockSpec((1, 2, n, TILE, width), lambda i: (1, 0, 0, i, 0))
        specs += [part_spec(n), other_spec, part_spec(n)]
    key_grad, value_grad = call(
        key_end_kernel,
        tokens // TILE,
        [smem, kv_tile, at_rest(1, width), row_spec, row_spec] + specs,
        [kv_tile] * 2,
        [sds((tokens, groups, width), bf16)] * 2,
        [pltpu.VMEM((2, TILE * groups, width), f32)],
        (8 * mib, 4 * mib),
    )(flag, keys, key_gain[None, :], cos, sin, *ends)
    return query_grad, key_grad, value_grad, gains[0], gains[1]


def solution(mesh):
    wide = P("seq", "kv", None)
    return jax.shard_map(
        body,
        mesh=mesh,
        in_specs=(wide, wide, wide, wide, P("seq"), P(), P()),
        out_specs=(wide, wide, wide, P(), P()),
        check_vma=False,
    )
```
